512 devices in a mesh: ctx: 64 (over z, x, core), grp: 8 (over y).
Axes of the slice: x: 4, y: 8, z: 8, core: 2. Of those that a mesh axis runs over, the one named last changes fastest.
Arguments:
- query: bfloat16 [8192, 8192], P('ctx', 'grp'), may hold values from -32 to 32, as said below
- key_in: bfloat16 [8192, 8192], P('ctx', 'grp'), may hold values from -6 to 6
- value: bfloat16 [8192, 8192], P('ctx', 'grp'), may hold values from -6 to 6
- filt: bfloat16 [1024, 512], P('ctx', 'grp'), may hold values from -2 to 2, as said below
- gain: bfloat16 [8192], P('grp'), may hold values from 0.099609375 to 1.8984375
- lengths: int32 [32], replicated, may hold values from 1 to 1024, 8192 in all
Outputs:
- normed: bfloat16 [8192, 8192], P('ctx', 'grp')
The draws below stay inside these ranges and needn't reach their ends.
Inputs may be any that keep to these rules, and one draw needn't show every extreme that they name: The lengths sum to 8192, and one document has exactly 1024 tokens. `query`: gate values of order one. `filt`: filter taps of order one or less.
All inputs are finite; a program needn't handle non-finite values.
Results may differ from the reference program's by a relative error of at most 0.0049.
Values may be sent and summed in bfloat16 or wider, within the bound.
A program may use at most 64 MiB of HBM per device.

```python
import math
import jax
import jax.numpy as jnp
import numpy as np
from jax import lax

D = 8192
TOK_DEV = 128
DOC_BLOCKS = 8
TOKENS = 8192
DOCMAX = 1024
FILT = 1024
GROUPS = 512
NDOCS = 32
N_CTX = 64


def draw_query(key, part):
    first, second, third = jax.random.split(jax.random.fold_in(key, 31), 3)
    matrix_col_number = jnp.arange(D, dtype=jnp.float32)[None, :] / (D - 1)
    columns = 4.0 ** matrix_col_number * jnp.exp(jax.random.uniform(first, (1, D), minval=-0.69, maxval=0.69))
    base = jnp.clip(jax.random.normal(second, (TOKENS, D)), -4.0, 4.0)
    rows_scale = jnp.exp(jax.random.uniform(third, (TOKENS, 1), minval=0.0, maxval=2.3))
    return jnp.clip(base * columns * rows_scale * 0.1, -32.0, 32.0).astype(jnp.bfloat16)


def draw_filt(key, part):
    first, second, third = jax.random.split(jax.random.fold_in(key, 57), 3)
    kernel_offset = jnp.arange(FILT, dtype=jnp.int32)[:, None]
    falloff_speeds = jnp.exp(jax.random.uniform(first, (1, GROUPS), minval=jnp.log(1.0 / (4.0 * FILT)), maxval=jnp.log(1.0 / 30.0)))
    spots = jax.random.randint(second, (4,), 1, FILT)
    entry_total = jnp.sum((kernel_offset[:, :, None] >= spots[None, None, :]).astype(jnp.float32), axis=2)
    span_size = 0.6 ** entry_total
    gaussian_jitter = jnp.clip(jax.random.normal(third, (FILT, GROUPS)), -4.0, 4.0)
    kernel_weights = gaussian_jitter * jnp.exp(-kernel_offset.astype(jnp.float32) * falloff_speeds) * span_size * 0.4
    return jnp.clip(kernel_weights, -2.0, 2.0).astype(jnp.bfloat16)


def block_levels(rng, shape, pieces, least, high):
    loudness, own = 1.0, jax.random.fold_in(rng, 6)
    for dim, shards_of in pieces:
        heights = jnp.exp(jax.random.uniform(jax.random.fold_in(own, dim), (shards_of,), jnp.float32, least / len(pieces), high / len(pieces)))
        loudness = loudness * jnp.repeat(heights, shape[dim] // shards_of).reshape([-1 if axis == dim else 1 for axis in range(len(shape))])
    return loudness


def profile(amount, total, limit, slope):
    loads = [(1 << 20) // math.isqrt(rank ** slope) + 1 for rank in range(2, amount + 1)]
    spare, given = total - limit - (amount - 1), [1] * (amount - 1)
    while spare > 0:
        free = [i for i in range(amount - 1) if given[i] < limit]
        mass, remaining = sum([loads[i] for i in free]), spare
        for i in free:
            addition = min(limit - given[i], max(1, remaining * loads[i] // mass), spare)
            given[i] = given[i] + addition
            spare = spare - addition
    return np.array([limit] + given)


def ragged_sizes(stream_key, amount, total, reach, slope):
    if amount == 2:
        one = jax.random.randint(stream_key, (), max(1, total - reach), min(reach, total - 1) + 1)
        return jnp.stack([one, total - one])
    sizes = jnp.asarray(profile(amount, total, reach, slope), jnp.int32)
    pairs = (amount - 1) // 2
    source_of, taker = sizes[1:1 + 2 * pairs:2], sizes[2:2 + 2 * pairs:2]
    margin = jnp.minimum(source_of - 1, reach - taker)
    shifted = jax.random.randint(jax.random.fold_in(stream_key, 1), (pairs,), 0, 1 << 20) % (margin + 1)
    sizes = sizes.at[1:1 + 2 * pairs:2].set(source_of - shifted).at[2:2 + 2 * pairs:2].set(taker + shifted)
    return sizes[jax.random.permutation(jax.random.fold_in(stream_key, 2), amount)]


def normal_values(rng, shape, scale, bound, shards=(), kind=jnp.bfloat16):
    drawn = jax.random.normal(rng, shape, jnp.float32) * scale
    if len(shards) > 0:
        drawn = block_levels(rng, shape, shards, -0.22, 0.18) * drawn
    return jnp.clip(drawn, min=-bound, max=bound).astype(kind)


def setup_inputs(seed: int = 0) -> dict:
    splits = jax.random.split(jax.random.key(seed), 7)
    query = draw_query(jax.random.fold_in(splits[6], 71), 0)
    key_in = normal_values(splits[1], (TOKENS, D), 1.0, 6.0, ((0, 64), (1, 8)))
    value = normal_values(splits[2], (TOKENS, D), 1.0, 6.0, ((0, 64), (1, 8)))
    filt = draw_filt(jax.random.fold_in(splits[6], 71), 0)
    gain = jnp.clip(1.0 + 0.18 * jax.random.normal(splits[4], (D,), jnp.float32), 0.099609375, 1.8984375).astype(jnp.bfloat16)
    lengths = ragged_sizes(splits[5], NDOCS, TOKENS, DOCMAX, 2).astype(jnp.int32)
    return dict(query=query, key_in=key_in, value=value, filt=filt, gain=gain, lengths=lengths)


def doc_numbers(lengths, first, entry_total):
    ends = jnp.cumsum(lengths).astype(jnp.int32)
    where = (first + lax.iota(jnp.int32, entry_total)).astype(jnp.int32)
    return lax.optimization_barrier(jnp.sum((ends[None, :] <= where[:, None]).astype(jnp.int32), axis=1)).astype(jnp.int32)

def band(filt, shift, rows):
    index = lax.iota(jnp.int32, rows)
    kernel_offset = (shift * rows + index[:, None] - index[None, :]).astype(jnp.int32)
    inside = (kernel_offset >= 0) & (kernel_offset < filt.shape[0])
    picked = jnp.take(filt, jnp.clip(kernel_offset, 0, filt.shape[0] - 1), axis=0)
    return jnp.where(inside[:, :, None], picked, jnp.zeros_like(picked))

def apply_band(kern, source):
    rows, width = source.shape
    groups = kern.shape[2]
    grouped = source.reshape(rows, groups, width // groups).astype(jnp.float32)
    out = jnp.einsum('tsg,sgc->tgc', kern.astype(jnp.float32), grouped)
    return out.reshape(rows, width)

def reference(query, key_in, value, filt, gain, lengths):
    signal = (key_in.astype(jnp.float32) * value.astype(jnp.float32)).astype(jnp.bfloat16)
    kerns = [band(filt, shift, TOK_DEV) for shift in range(DOC_BLOCKS + 1)]
    docs = doc_numbers(lengths, 0, TOKENS)

    def one_block(block):
        start = (block * TOK_DEV).astype(jnp.int32)
        mine = lax.dynamic_slice_in_dim(docs, start, TOK_DEV)
        same = mine[:, None] == mine[None, :]
        here = lax.dynamic_slice_in_dim(signal, start, TOK_DEV, 0)
        diag = jnp.where(same[:, :, None], kerns[0], jnp.zeros_like(kerns[0]))
        total = apply_band(diag, here)
        first = mine[0]
        rowm = (mine == first).astype(jnp.float32)
        for shift in range(1, DOC_BLOCKS + 1):
            begin = start - shift * TOK_DEV
            safe = jnp.maximum(begin, 0).astype(jnp.int32)
            source = lax.dynamic_slice_in_dim(signal, safe, TOK_DEV, 0)
            preceding_tokens = lax.dynamic_slice_in_dim(docs, safe, TOK_DEV)
            cols = (preceding_tokens == first) & (begin >= 0)
            kern = kerns[shift]

            def work(source, cols, kern=kern):
                masked = jnp.where(cols[:, None], source, jnp.zeros_like(source))
                return apply_band(kern, masked) * rowm[:, None]

            def skip(source, cols):
                return jnp.zeros((TOK_DEV, D), jnp.float32)
            total = total + lax.cond(jnp.any(cols), work, skip, source, cols)
        return total
    conv = lax.map(one_block, jnp.arange(N_CTX, dtype=jnp.int32)).reshape(TOKENS, D)
    gated = query.astype(jnp.float32) * conv
    power = lax.optimization_barrier(jnp.sum(gated * gated, axis=1))
    scale = lax.rsqrt(power / D + 1e-05)
    return (gated * scale[:, None] * gain.astype(jnp.float32)[None, :]).astype(jnp.bfloat16)
```

```python
from functools import partial

import jax
import jax.numpy as jnp
from jax import lax
from jax.sharding import PartitionSpec as P

DOC_BLOCKS = 8


def passed_along(value, axis, steps):
    count = lax.axis_size(axis)
    leading, last = (max(0, -steps), min(count, count - steps))
    return lax.ppermute(value, axis, [(source, source + steps) for source in range(leading, last)])


def doc_numbers(lengths, first, entry_total):
    number = lax.iota(jnp.int32, lengths.shape[0])
    ends = jnp.sum(jnp.where(number[None, :] <= number[:, None], lengths[None, :], 0), axis=1)
    where = first + lax.iota(jnp.int32, entry_total)
    return jnp.sum((ends[None, :] <= where[:, None]).astype(jnp.int32), axis=1)


def band_rows(filt_rows, shift, rows):
    index = lax.iota(jnp.int32, rows)
    kernel_offset = shift * rows + index[:, None] - index[None, :]
    inside = (kernel_offset >= 0) & (kernel_offset < filt_rows.shape[1])
    picked = jnp.take(filt_rows, jnp.clip(kernel_offset, 0, filt_rows.shape[1] - 1), axis=1)
    return jnp.where(inside[None, :, :], picked, jnp.zeros_like(picked))


def apply_rows(kern, source):
    width, rows = source.shape
    groups = kern.shape[0]
    grouped = source.reshape(groups, width // groups, rows)
    out = jnp.einsum("gts,gcs->gct", kern, grouped, preferred_element_type=jnp.float32)
    return out.reshape(width, rows)


def far_term(filt_rows, shift, source, cols, rowm):
    kern = band_rows(filt_rows, shift, source.shape[1])
    masked = jnp.where(cols[None, :], source, jnp.zeros_like(source))
    return apply_rows(kern, masked) * rowm[None, :].astype(jnp.float32)


def zero_term(source, cols, rowm):
    return jnp.zeros(source.shape, jnp.float32)


def shards(query, key_in, value, filt, gain, lengths):
    rows, width = query.shape
    signal = (key_in.astype(jnp.float32) * value.astype(jnp.float32)).astype(jnp.bfloat16)
    full_filter = lax.all_gather(filt, "ctx", axis=0, tiled=True)
    filt_rows = full_filter.T
    start = lax.axis_index("ctx") * rows
    signal_rows = signal.T
    mine = doc_numbers(lengths, start, rows)
    same = mine[:, None] == mine[None, :]
    diag_kern = band_rows(filt_rows, 0, rows)
    diag_kern = jnp.where(same[None, :, :], diag_kern, jnp.zeros_like(diag_kern))
    conv_rows = apply_rows(diag_kern, signal_rows)
    first = mine[0]
    rowm = mine == first
    for shift in range(1, DOC_BLOCKS + 1):
        source = passed_along(signal_rows, "ctx", shift)
        begin = start - shift * rows
        preceding_tokens = doc_numbers(lengths, begin, rows)
        cols = (preceding_tokens == first) & (begin >= 0)
        conv_rows = conv_rows + lax.cond(
            jnp.any(cols), partial(far_term, filt_rows, shift), zero_term, source, cols, rowm
        )
    conv = conv_rows.T
    gated = query.astype(jnp.float32) * conv
    power = lax.psum(jnp.sum(gated * gated, axis=1), "grp")
    scale = lax.rsqrt(power / (width * lax.axis_size("grp")) + 1e-05)
    return (gated * scale[:, None] * gain.astype(jnp.float32)[None, :]).astype(jnp.bfloat16)


def solution(mesh):
    placed = (P("ctx", "grp"), P("ctx", "grp"), P("ctx", "grp"), P("ctx", "grp"), P("grp"), P())
    return jax.shard_map(
        shards, mesh=mesh, in_specs=placed, out_specs=P("ctx", "grp"), check_vma=False
    )
```

```python
from functools import partial

import jax
import jax.numpy as jnp
from jax import lax
from jax.experimental import pallas as pl
from jax.experimental.pallas import tpu as pltpu
from jax.sharding import PartitionSpec as P

LONGEST = 1024
EPS = 1e-05
MESH = pl.DeviceIdType.MESH
BF16, F32 = jnp.bfloat16, jnp.float32


def kernel(
    sizes, lengths_hbm, filt_hbm, gain_hbm, query, key_in, value, out,
    lengths, filt, gain, q, k_buf, v_buf, fpad, fsend, frecv, ff, xsend, xin, wfar, w0, srcmask, diagmask, xm,
    outbuf, cin, gated, pw, load_sem,
    f1_s, f1_r, f2_s, f2_r, x_s, x_r, h_s, h_r, o_s, o_r, p_s, p_r,
):
    per, planes, across, rows, width, taps, docs = sizes
    groups = filt.shape[1]
    mine, per_group = groups // per, width // groups
    wide = width // per
    me, y = lax.axis_index("ctx"), lax.axis_index("grp")
    z, j = me // per, me % per

    def at(plane, place):
        return (lax.rem(plane, planes) * per + lax.rem(place, per), y)

    loads = [
        pltpu.make_async_copy(src, dst, load_sem.at[i])
        for i, (src, dst) in enumerate((
            (key_in, k_buf), (value, v_buf), (query, q), (filt_hbm, filt), (lengths_hbm, lengths), (gain_hbm, gain)
        ))
    ]
    for load in loads:
        load.start()

    barrier = pltpu.get_barrier_semaphore()
    before = [at(z, j + d) for d in range(1, per)]
    before += [at(z + planes - 1, j + d) for d in range(per)]
    before += [at(z + d, j) for d in range(1, planes - 1)]
    before += [(me, lax.rem(y + d, across)) for d in range(1, across)]
    for device in before:
        pl.semaphore_signal(barrier, inc=1, device_id=device, device_id_type=MESH)

    fpad[...] = jnp.zeros_like(fpad)
    loads[3].wait()
    fpad[pl.ds(pl.multiple_of(j * taps, taps), taps), 0:groups] = filt[...].astype(F32)
    by_group = jnp.transpose(fpad[...])
    for d in range(per):
        fsend[d] = by_group[d * mine:(d + 1) * mine]

    loads[0].wait()
    loads[1].wait()
    for d in range(per):
        cols = slice(d * wide, (d + 1) * wide)
        signal = k_buf[:, cols].astype(F32) * v_buf[:, cols].astype(F32)
        xsend[d] = jnp.transpose(signal).astype(BF16)

    pl.semaphore_wait(barrier, len(before))

    def send(src, dst, send_sem, recv_sem, device):
        copy = pltpu.make_async_remote_copy(
            src_ref=src, dst_ref=dst, send_sem=send_sem, recv_sem=recv_sem, device_id=device, device_id_type=MESH
        )
        copy.start()
        return copy

    f1, halo, plane = [], [], []
    for d in range(1, per):
        to = lax.rem(j + d, per)
        f1.append(send(fsend.at[to], frecv.at[j], f1_s.at[d], f1_r.at[d], at(z, j + d)))
    for d in range(per):
        to = lax.rem(j + d, per)
        halo.append(send(xsend.at[to], xin.at[j], h_s.at[d], h_r.at[d], at(z + 1, j + d)))
        if d:
            plane.append(send(xsend.at[to], xin.at[per + j], x_s.at[d], x_r.at[d], at(z, j + d)))
    xin[per + j] = xsend[j]
    frecv[j] = fsend[j]

    loads[4].wait()
    base = z * (per * rows)
    block = lax.broadcasted_iota(jnp.int32, (per, rows), 0)
    lane = lax.broadcasted_iota(jnp.int32, (per, rows), 1)
    head = base + block * rows
    token = head + lane
    end, start, first = jnp.int32(0), jnp.zeros_like(token), jnp.zeros_like(token)
    for m in range(docs):
        end = end + lengths[m]
        start = jnp.where(end <= token, end, start)
        first = jnp.where(end <= head, end, first)
    reach = (start < head).astype(F32)
    for lag in range(1, per + 1):
        keep = (token - lag * rows >= first).astype(F32)
        for a in range(per):
            srcmask[a * per + lag - 1] = jnp.broadcast_to(keep[a:a + 1], (per_group, rows)).astype(BF16)
    source = lax.broadcasted_iota(jnp.int32, (rows, rows), 0)
    target = lax.broadcasted_iota(jnp.int32, (rows, rows), 1)
    within = start - head
    for a in range(per):
        diagmask[a] = (source >= within[a:a + 1]).astype(F32).astype(BF16)

    for copy in f1:
        copy.wait_recv()
    taps_here = frecv[0]
    for d in range(1, per):
        taps_here = taps_here + frecv[d]
    ff[z] = taps_here
    f2 = [
        send(ff.at[z], ff.at[z], f2_s.at[d], f2_r.at[d], at(z + d, j)) for d in range(1, planes)
    ]
    for copy in f2:
        copy.wait_recv()

    causal = target >= source

    def build(g, carry):
        last = None
        for lag in range(min(per, planes)):
            row = jnp.broadcast_to(ff[lag, pl.ds(g, 1), :], (rows, rows))
            turned = pltpu.roll(row, 0, 1, stride=1, stride_axis=0)
            if lag == 0:
                w0[g] = jnp.where(causal, turned, 0.0).astype(BF16)
            else:
                wfar[g, (lag - 1) * rows:lag * rows, :] = jnp.where(causal, turned, last).astype(BF16)
            last = turned
        for lag in range(min(per, planes), per + 1):
            ended = jnp.where(causal, 0.0, last) if lag == planes else jnp.zeros_like(last)
            wfar[g, (lag - 1) * rows:lag * rows, :] = ended.astype(BF16)
        return carry

    lax.fori_loop(0, mine, build, 0)

    for copy in plane + halo:
        copy.wait_recv()

    def convolve(g, carry):
        part = pl.ds(pl.multiple_of(g * per_group, per_group), per_group)
        for a in range(per):
            for lag in range(1, per + 1):
                xm[a * per_group:(a + 1) * per_group, (lag - 1) * rows:lag * rows] = (
                    xin[per + a - lag, part, :] * srcmask[a * per + lag - 1]
                )
        far = jnp.dot(xm[...], wfar[g], preferred_element_type=F32)
        near = w0[g]
        for a in range(per):
            own = jnp.dot(xin[per + a, part, :], near * diagmask[a], preferred_element_type=F32)
            conv = far[a * per_group:(a + 1) * per_group] * reach[a:a + 1] + own
            outbuf[a, part, :] = conv.astype(BF16)
        return carry

    lax.fori_loop(0, mine, convolve, 0)

    back = []
    for d in range(1, per):
        to = lax.rem(j + d, per)
        back.append(send(outbuf.at[to], cin.at[j], o_s.at[d], o_r.at[d], at(z, j + d)))
    cin[j] = outbuf[j]
    loads[2].wait()
    total = jnp.zeros((rows, wide), F32)
    for d in range(per):
        if d:
            back[d - 1].wait_recv()
        origin = lax.rem(j + per - d, per)
        cols = pl.ds(pl.multiple_of(origin * wide, wide), wide)
        conv = jnp.transpose(cin[origin].astype(F32))
        some = q[:, cols].astype(F32) * conv
        gated[:, cols] = some
        total = total + some * some
    power = jnp.sum(jnp.transpose(total), axis=0, keepdims=True)
    pw[y] = jnp.broadcast_to(power, pw.shape[1:])
    shared = [
        send(pw.at[y], pw.at[y], p_s.at[d], p_r.at[d], (me, lax.rem(y + d, across))) for d in range(1, across)
    ]
    for copy in shared:
        copy.wait_recv()
    power = pw[0]
    for d in range(1, across):
        power = power + pw[d]
    scale = lax.rsqrt(power / (width * across) + EPS)
    scale = jnp.transpose(jnp.broadcast_to(scale[0:1], (rows, rows)))
    loads[5].wait()
    for d in range(per):
        cols = slice(d * wide, (d + 1) * wide)
        weight = gain[cols].astype(F32).reshape(1, wide)
        out[:, cols] = (gated[:, cols] * scale * weight).astype(BF16)
    for copy in f1 + halo + plane + f2 + back + shared:
        copy.wait_send()


def shards(query, key_in, value, filt, gain, lengths):
    rows, width = query.shape
    taps, groups = filt.shape
    per = LONGEST // rows
    planes, across = lax.axis_size("ctx") // per, lax.axis_size("grp")
    mine, wide = groups // per, width // per
    sizes = (per, planes, across, rows, width, taps, lengths.shape[0])
    vmem, dma = pltpu.VMEM, pltpu.SemaphoreType.DMA
    return pl.pallas_call(
        partial(kernel, sizes),
        out_shape=jax.ShapeDtypeStruct((rows, width), BF16),
        in_specs=[pl.BlockSpec(memory_space=pltpu.HBM)] * 6,
        out_specs=pl.BlockSpec(memory_space=vmem),
        scratch_shapes=[
            pltpu.SMEM(lengths.shape, jnp.int32),
            vmem(filt.shape, BF16),
            vmem(gain.shape, BF16),
            vmem((rows, width), BF16),
            vmem((rows, width), BF16),
            vmem((rows, width), BF16),
            vmem((rows, rows), F32),
            vmem((per, mine, rows), F32),
            vmem((per, mine, rows), F32),
            vmem((planes, mine, rows), F32),
            vmem((per, wide, rows), BF16),
            vmem((2 * per, wide, rows), BF16),
            vmem((mine, per * rows, rows), BF16),
            vmem((mine, rows, rows), BF16),
            vmem((per * per, width // groups, rows), BF16),
            vmem((per, rows, rows), BF16),
            vmem((per * (width // groups), per * rows), BF16),
            vmem((per, wide, rows), BF16),
            vmem((per, wide, rows), BF16),
            vmem((rows, width), F32),
            vmem((across, 8, rows), F32),
            dma((6,)),
            dma((per,)), dma((per,)),
            dma((planes,)), dma((planes,)),
            dma((per,)), dma((per,)),
            dma((per,)), dma((per,)),
            dma((per,)), dma((per,)),
            dma((across,)), dma((across,)),
        ],
        compiler_params=pltpu.CompilerParams(
            collective_id=0, has_side_effects=True, vmem_limit_bytes=65000 * 1024
        ),
    )(lengths, filt, gain, query, key_in, value)


def solution(mesh):
    placed = (P("ctx", "grp"), P("ctx", "grp"), P("ctx", "grp"), P("ctx", "grp"), P("grp"), P())
    return jax.shard_map(
        shards, mesh=mesh, in_specs=placed, out_specs=P("ctx", "grp"), check_vma=False
    )
```

```python
from functools import partial

import jax
import jax.numpy as jnp
from jax import lax
from jax.experimental import pallas as pl
from jax.experimental.pallas import tpu as pltpu
from jax.sharding import PartitionSpec as P

LONGEST = 1024
EARLY = 3
EPS = 1e-05
MESH = pl.DeviceIdType.MESH
BF16, F32 = jnp.bfloat16, jnp.float32


def kernel(
    sizes, lengths_hbm, filt_hbm, gain_hbm, query, key_in, value, out,
    lengths, filt, gain, q, k_buf, v_buf, fpad, fsend, frecv, ff, turned, xsend, xin, wfar, w0, diagmask, xm,
    acc, outbuf, cin, gated, pw, load_sem,
    f1_s, f1_r, f2_s, f2_r, x_s, x_r, h_s, h_r, o_s, o_r, p_s, p_r, hello,
):
    per, planes, across, rows, width, taps, docs = sizes
    groups = filt.shape[1]
    mine, per_group = groups // per, width // groups
    wide = width // per
    me, y = lax.axis_index("ctx"), lax.axis_index("grp")
    z, j = me // per, me % per
    chip, core = j // 2, j % 2
    chips = per // 2

    def place(dx, dc):
        return lax.rem(chip + dx, chips) * 2 + lax.rem(core + dc, 2)

    def in_plane(to):
        return (z * per + to, y)

    def in_column(d):
        return (lax.rem(z + d, planes) * per + j, y)

    order = list(dict.fromkeys([0] + [dx for pair in zip(range(1, chips), range(chips - 1, 0, -1)) for dx in pair]))
    peers = [(dx, dc, dx * 2 + dc) for dx in order for dc in (0, 1)][1:]

    loads = [
        pltpu.make_async_copy(src, dst, load_sem.at[i])
        for i, (src, dst) in enumerate((
            (filt_hbm, filt), (key_in, k_buf), (value, v_buf), (lengths_hbm, lengths), (query, q), (gain_hbm, gain)
        ))
    ]
    for load in loads:
        load.start()

    barrier = pltpu.get_barrier_semaphore()

    def greet(device):
        pl.semaphore_signal(barrier, inc=1, device_id=device, device_id_type=MESH)

    for dx, dc, _ in peers:
        greet(in_plane(place(dx, dc)))
    for d in range(1, across):
        greet((me, lax.rem(y + d, across)))
    greet(in_column(planes - 1))
    for d in range(1, planes - 1):
        pl.when(z + d < planes)(partial(greet, in_column(d)))
    greeted = (per - 1) + (across - 1) + z + jnp.where(z < planes - 1, 1, 0)

    fpad[...] = jnp.zeros_like(fpad)
    loads[0].wait()
    fpad[pl.ds(pl.multiple_of(j * taps, taps), taps), 0:groups] = filt[...].astype(F32)
    by_group = jnp.transpose(fpad[...])
    for d in range(per):
        fsend[d] = by_group[d * mine:(d + 1) * mine]

    loads[1].wait()
    loads[2].wait()
    for b in range(per):
        cols = slice(b * wide, (b + 1) * wide)
        signal = k_buf[:, cols].astype(F32) * v_buf[:, cols].astype(F32)
        xsend[b] = jnp.transpose(signal).astype(BF16)

    pl.semaphore_wait(barrier, greeted)

    def copy_to(src, dst, send_sem, recv_sem, device):
        return pltpu.make_async_remote_copy(
            src_ref=src, dst_ref=dst, send_sem=send_sem, recv_sem=recv_sem, device_id=device, device_id_type=MESH
        )

    def send(*what):
        copy = copy_to(*what)
        copy.start()
        return copy

    for d in range(1, planes):
        @pl.when(z >= d)
        def _():
            pl.semaphore_signal(hello.at[d], inc=1, device_id=in_column(planes - d), device_id_type=MESH)

    f1, plane = [], []
    for dx, dc, n in peers:
        to = place(dx, dc)
        f1.append(send(fsend.at[to], frecv.at[j], f1_s.at[n], f1_r.at[n], in_plane(to)))
    for dx, dc, n in peers:
        to = place(dx, dc)
        plane.append(send(xsend.at[to], xin.at[per + j], x_s.at[n], x_r.at[n], in_plane(to)))
    halo = [copy_to(xsend.at[j], xin.at[j], h_s.at[0], h_r.at[0], in_column(1))]
    for dx, dc, n in peers:
        origin = place(chips - dx, 2 - dc)
        halo.append(copy_to(xin.at[per + origin], xin.at[origin], h_s.at[n], h_r.at[n], in_column(1)))
    pl.when(z < planes - 1)(halo[0].start)
    xin[per + j] = xsend[j]
    frecv[j] = fsend[j]

    @pl.when(z == 0)
    def _():
        xin[0:per] = jnp.zeros((per, wide, rows), BF16)

    loads[3].wait()
    base = z * (per * rows)
    block = lax.broadcasted_iota(jnp.int32, (per, rows), 0)
    lane = lax.broadcasted_iota(jnp.int32, (per, rows), 1)
    ahead = base + block * rows
    token = ahead + lane
    end, start, first = jnp.int32(0), jnp.zeros_like(token), jnp.zeros_like(token)
    for m in range(docs):
        end = end + lengths[m]
        start = jnp.where(end <= token, end, start)
        first = jnp.where(end <= ahead, end, first)

    for copy in f1:
        copy.wait_recv()
    taps_here = frecv[0]
    for d in range(1, per):
        taps_here = taps_here + frecv[d]
    ff[z] = taps_here
    f2 = [copy_to(ff.at[z], ff.at[z], f2_s.at[d], f2_r.at[d], in_column(d)) for d in range(1, planes)]
    for d in range(1, planes):
        pl.when(z + d >= planes)(f2[d - 1].start)

    for copy, following in zip(plane, halo[1:]):
        copy.wait_recv()
        pl.when(z < planes - 1)(following.start)

    reach = jnp.concatenate(
        [jnp.broadcast_to((start < ahead).astype(F32)[a:a + 1], (per_group, rows)) for a in range(per)], axis=0
    )
    source = lax.broadcasted_iota(jnp.int32, (rows, rows), 0)
    target = lax.broadcasted_iota(jnp.int32, (rows, rows), 1)
    causal = target >= source
    within = start - ahead
    for a in range(per):
        diagmask[a] = (source >= within[a:a + 1]).astype(F32).astype(BF16)

    for d in range(1, planes):
        @pl.when(z + d < planes)
        def _():
            pl.semaphore_wait(hello.at[d], 1)
            f2[d - 1].start()

    def take(other):
        @pl.when(z != other)
        def _():
            d = lax.rem(z - other + planes, planes)
            copy_to(ff.at[other], ff.at[other], f2_s.at[d], f2_r.at[d], in_column(d)).wait_recv()

    def build(lag, g, carry):
        if lag < planes:
            row = jnp.broadcast_to(ff[lag, pl.ds(g, 1), :], (rows, rows))
            now = pltpu.roll(row, 0, 1, stride=1, stride_axis=0)
        else:
            now = jnp.zeros((rows, rows), F32)
        if lag == 0:
            w0[g] = jnp.where(causal, now, 0.0).astype(BF16)
        else:
            wfar[g, (lag - 1) * rows:lag * rows, :] = jnp.where(causal, now, turned[g]).astype(BF16)
        turned[g] = now
        return carry

    def part(g):
        return pl.ds(pl.multiple_of(g * per_group, per_group), per_group)

    masks = [(token - lag * rows >= first).astype(F32) for lag in range(1, per + 1)]

    def gather(g, carry):
        for a in range(per):
            for lag in range(1, per + 1):
                keep = jnp.broadcast_to(masks[lag - 1][a:a + 1], (per_group, rows)).astype(BF16)
                xm[g, a * per_group:(a + 1) * per_group, (lag - 1) * rows:lag * rows] = (
                    xin[per + a - lag, part(g), :] * keep
                )
        return carry

    def begin(g, carry):
        far = jnp.dot(xm[g, :, 0:EARLY * rows], wfar[g, 0:EARLY * rows, :], preferred_element_type=F32) * reach
        near = w0[g]
        for a in range(per):
            own = jnp.dot(xin[per + a, part(g), :], near * diagmask[a], preferred_element_type=F32)
            here = slice(a * per_group, (a + 1) * per_group)
            acc[g, here] = far[here] + own
        return carry

    def finish(g, carry):
        far = jnp.dot(xm[g, :, EARLY * rows:], wfar[g, EARLY * rows:, :], preferred_element_type=F32)
        conv = (far * reach + acc[g]).astype(BF16)
        for a in range(per):
            outbuf[a, part(g), :] = conv[a * per_group:(a + 1) * per_group]
        return carry

    for lag in range(EARLY + 1):
        if lag < planes:
            take(lag)
        lax.fori_loop(0, mine, partial(build, lag), 0, unroll=True)
    for copy in halo:
        pl.when(z > 0)(copy.wait_recv)
    lax.fori_loop(0, mine, gather, 0, unroll=True)
    lax.fori_loop(0, mine, begin, 0, unroll=True)
    for lag in range(EARLY + 1, per + 1):
        if lag < planes:
            take(lag)
        lax.fori_loop(0, mine, partial(build, lag), 0, unroll=True)
    lax.fori_loop(0, mine, finish, 0, unroll=True)

    back = []
    for dx, dc, n in peers:
        to = place(dx, dc)
        back.append(send(outbuf.at[to], cin.at[j], o_s.at[n], o_r.at[n], in_plane(to)))
    cin[j] = outbuf[j]
    loads[4].wait()
    total = jnp.zeros((rows, wide), F32)
    for copy, (dx, dc, n) in zip([None] + back, [(0, 0, 0)] + peers):
        if copy is not None:
            copy.wait_recv()
        origin = place(chips - dx, 2 - dc)
        cols = pl.ds(pl.multiple_of(origin * wide, wide), wide)
        conv = jnp.transpose(cin[origin].astype(F32))
        some = q[:, cols].astype(F32) * conv
        gated[:, cols] = some
        total = total + some * some
    power = jnp.sum(jnp.transpose(total), axis=0, keepdims=True)
    pw[y] = jnp.broadcast_to(power, pw.shape[1:])
    shared = [
        send(pw.at[y], pw.at[y], p_s.at[d], p_r.at[d], (me, lax.rem(y + d, across))) for d in range(1, across)
    ]
    for copy in shared:
        copy.wait_recv()
    power = pw[0]
    for d in range(1, across):
        power = power + pw[d]
    scale = lax.rsqrt(power / (width * across) + EPS)
    scale = jnp.transpose(jnp.broadcast_to(scale[0:1], (rows, rows)))
    loads[5].wait()
    for d in range(per):
        cols = slice(d * wide, (d + 1) * wide)
        weight = gain[cols].astype(F32).reshape(1, wide)
        out[:, cols] = (gated[:, cols] * scale * weight).astype(BF16)
    for copy in f1 + f2 + plane + back + shared:
        copy.wait_send()
    for copy in halo:
        pl.when(z < planes - 1)(copy.wait_send)


def shards(query, key_in, value, filt, gain, lengths):
    rows, width = query.shape
    taps, groups = filt.shape
    per = LONGEST // rows
    planes, across = lax.axis_size("ctx") // per, lax.axis_size("grp")
    mine, wide = groups // per, width // per
    sizes = (per, planes, across, rows, width, taps, lengths.shape[0])
    vmem, dma = pltpu.VMEM, pltpu.SemaphoreType.DMA
    return pl.pallas_call(
        partial(kernel, sizes),
        out_shape=jax.ShapeDtypeStruct((rows, width), BF16),
        in_specs=[pl.BlockSpec(memory_space=pltpu.HBM)] * 6,
        out_specs=pl.BlockSpec(memory_space=vmem),
        scratch_shapes=[
            pltpu.SMEM(lengths.shape, jnp.int32),
            vmem(filt.shape, BF16),
            vmem(gain.shape, BF16),
            vmem((rows, width), BF16),
            vmem((rows, width), BF16),
            vmem((rows, width), BF16),
            vmem((rows, rows), F32),
            vmem((per, mine, rows), F32),
            vmem((per, mine, rows), F32),
            vmem((planes, mine, rows), F32),
            vmem((mine, rows, rows), F32),
            vmem((per, wide, rows), BF16),
            vmem((2 * per, wide, rows), BF16),
            vmem((mine, per * rows, rows), BF16),
            vmem((mine, rows, rows), BF16),
            vmem((per, rows, rows), BF16),
            vmem((mine, per * (width // groups), per * rows), BF16),
            vmem((mine, per * (width // groups), rows), F32),
            vmem((per, wide, rows), BF16),
            vmem((per, wide, rows), BF16),
            vmem((rows, width), F32),
            vmem((across, 8, rows), F32),
            dma((6,)),
            dma((per,)), dma((per,)),
            dma((planes,)), dma((planes,)),
            dma((per,)), dma((per,)),
            dma((per,)), dma((per,)),
            dma((per,)), dma((per,)),
            dma((across,)), dma((across,)),
            pltpu.SemaphoreType.REGULAR((planes,)),
        ],
        compiler_params=pltpu.CompilerParams(
            collective_id=0, has_side_effects=True, vmem_limit_bytes=65000 * 1024
        ),
    )(lengths, filt, gain, query, key_in, value)


def solution(mesh):
    placed = (P("ctx", "grp"), P("ctx", "grp"), P("ctx", "grp"), P("ctx", "grp"), P("grp"), P())
    return jax.shard_map(
        shards, mesh=mesh, in_specs=placed, out_specs=P("ctx", "grp"), check_vma=False
    )
```

```python
from functools import partial

import jax
import jax.numpy as jnp
from jax import lax
from jax.experimental import pallas as pl
from jax.experimental.pallas import tpu as pltpu
from jax.sharding import PartitionSpec as P

LONGEST = 1024
EARLY = 3
EPS = 1e-05
MESH = pl.DeviceIdType.MESH
BF16, F32 = jnp.bfloat16, jnp.float32


def kernel(
    sizes, lengths_hbm, filt_hbm, gain_hbm, query, key_in, value, out,
    lengths, filt, gain, q_buf, k_buf, v_buf, fpad, fsend, frecv, ff, turned, xsend, xin, qsend, qin, wfar, w0, diagmask, xm,
    acc, outbuf, cin, gated, pw, psend, precv, load_sem,
    f1_s, f1_r, f2_s, f2_r, x_s, x_r, q_s, q_r, h_s, h_r, o_s, o_r, p_s, p_r, t_s, t_r, hello,
):
    per, planes, across, rows, width, taps, docs = sizes
    groups = filt.shape[1]
    mine, per_group = groups // per, width // groups
    wide = width // per
    me, y = lax.axis_index("ctx"), lax.axis_index("grp")
    z, j = me // per, me % per
    chip, core = j // 2, j % 2
    chips = per // 2

    def place(dx, dc):
        return lax.rem(chip + dx, chips) * 2 + lax.rem(core + dc, 2)

    def in_plane(to):
        return (z * per + to, y)

    def in_column(d):
        return (lax.rem(z + d, planes) * per + j, y)

    order = list(dict.fromkeys([0] + [dx for pair in zip(range(1, chips), range(chips - 1, 0, -1)) for dx in pair]))
    peers = [(dx, dc, dx * 2 + dc) for dx in order for dc in (0, 1)][1:]

    loads = [
        pltpu.make_async_copy(src, dst, load_sem.at[i])
        for i, (src, dst) in enumerate((
            (filt_hbm, filt), (key_in, k_buf), (value, v_buf), (lengths_hbm, lengths), (query, q_buf), (gain_hbm, gain)
        ))
    ]
    for load in loads:
        load.start()

    barrier = pltpu.get_barrier_semaphore()

    def greet(device):
        pl.semaphore_signal(barrier, inc=1, device_id=device, device_id_type=MESH)

    for dx, dc, _ in peers:
        greet(in_plane(place(dx, dc)))
    for d in range(1, across):
        greet((me, lax.rem(y + d, across)))
    greet(in_column(planes - 1))
    for d in range(1, planes - 1):
        pl.when(z + d < planes)(partial(greet, in_column(d)))
    greeted = (per - 1) + (across - 1) + z + jnp.where(z < planes - 1, 1, 0)

    fpad[...] = jnp.zeros_like(fpad)
    loads[0].wait()
    fpad[pl.ds(pl.multiple_of(j * taps, taps), taps), 0:groups] = filt[...].astype(F32)
    by_group = jnp.transpose(fpad[...])
    for d in range(per):
        fsend[d] = by_group[d * mine:(d + 1) * mine]

    loads[1].wait()
    loads[2].wait()
    for b in range(per):
        cols = slice(b * wide, (b + 1) * wide)
        signal = k_buf[:, cols].astype(F32) * v_buf[:, cols].astype(F32)
        xsend[b] = jnp.transpose(signal).astype(BF16)

    pl.semaphore_wait(barrier, greeted)

    def copy_to(src, dst, send_sem, recv_sem, device):
        return pltpu.make_async_remote_copy(
            src_ref=src, dst_ref=dst, send_sem=send_sem, recv_sem=recv_sem, device_id=device, device_id_type=MESH
        )

    def send(*what):
        copy = copy_to(*what)
        copy.start()
        return copy

    for d in range(1, planes):
        @pl.when(z >= d)
        def _():
            pl.semaphore_signal(hello.at[d], inc=1, device_id=in_column(planes - d), device_id_type=MESH)

    f1, plane = [], []
    for dx, dc, n in peers:
        to = place(dx, dc)
        f1.append(send(fsend.at[to], frecv.at[j], f1_s.at[n], f1_r.at[n], in_plane(to)))
    for dx, dc, n in peers:
        to = place(dx, dc)
        plane.append(send(xsend.at[to], xin.at[per + j], x_s.at[n], x_r.at[n], in_plane(to)))
    halo = [copy_to(xsend.at[j], xin.at[j], h_s.at[0], h_r.at[0], in_column(1))]
    for dx, dc, n in peers:
        origin = place(chips - dx, 2 - dc)
        halo.append(copy_to(xin.at[per + origin], xin.at[origin], h_s.at[n], h_r.at[n], in_column(1)))
    pl.when(z < planes - 1)(halo[0].start)
    xin[per + j] = xsend[j]
    frecv[j] = fsend[j]

    @pl.when(z == 0)
    def _():
        xin[0:per] = jnp.zeros((per, wide, rows), BF16)

    loads[3].wait()
    base = z * (per * rows)
    block = lax.broadcasted_iota(jnp.int32, (per, rows), 0)
    lane = lax.broadcasted_iota(jnp.int32, (per, rows), 1)
    ahead = base + block * rows
    token = ahead + lane
    end, start, first = jnp.int32(0), jnp.zeros_like(token), jnp.zeros_like(token)
    for m in range(docs):
        end = end + lengths[m]
        start = jnp.where(end <= token, end, start)
        first = jnp.where(end <= ahead, end, first)

    for copy in f1:
        copy.wait_recv()
    taps_here = frecv[0]
    for d in range(1, per):
        taps_here = taps_here + frecv[d]
    ff[z] = taps_here
    f2 = [copy_to(ff.at[z], ff.at[z], f2_s.at[d], f2_r.at[d], in_column(d)) for d in range(1, planes)]
    for d in range(1, planes):
        pl.when(z + d >= planes)(f2[d - 1].start)

    for copy, following in zip(plane, halo[1:]):
        copy.wait_recv()
        pl.when(z < planes - 1)(following.start)

    loads[4].wait()
    asked = []
    for b in range(per):
        cols = slice(b * wide, (b + 1) * wide)
        qsend[b] = jnp.transpose(q_buf[:, cols].astype(F32)).astype(BF16)
    for dx, dc, n in peers:
        to = place(dx, dc)
        asked.append(send(qsend.at[to], qin.at[j], q_s.at[n], q_r.at[n], in_plane(to)))
    qin[j] = qsend[j]

    reach = jnp.concatenate(
        [jnp.broadcast_to((start < ahead).astype(F32)[a:a + 1], (per_group, rows)) for a in range(per)], axis=0
    )
    source = lax.broadcasted_iota(jnp.int32, (rows, rows), 0)
    target = lax.broadcasted_iota(jnp.int32, (rows, rows), 1)
    causal = target >= source
    within = start - ahead
    for a in range(per):
        diagmask[a] = (source >= within[a:a + 1]).astype(F32).astype(BF16)

    for d in range(1, planes):
        @pl.when(z + d < planes)
        def _():
            pl.semaphore_wait(hello.at[d], 1)
            f2[d - 1].start()

    def take(other):
        @pl.when(z != other)
        def _():
            d = lax.rem(z - other + planes, planes)
            copy_to(ff.at[other], ff.at[other], f2_s.at[d], f2_r.at[d], in_column(d)).wait_recv()

    def build(lag, g, carry):
        if lag < planes:
            row = jnp.broadcast_to(ff[lag, pl.ds(g, 1), :], (rows, rows))
            now = pltpu.roll(row, 0, 1, stride=1, stride_axis=0)
        else:
            now = jnp.zeros((rows, rows), F32)
        if lag == 0:
            w0[g] = jnp.where(causal, now, 0.0).astype(BF16)
        else:
            wfar[g, (lag - 1) * rows:lag * rows, :] = jnp.where(causal, now, turned[g]).astype(BF16)
        turned[g] = now
        return carry

    def part(g):
        return pl.ds(pl.multiple_of(g * per_group, per_group), per_group)

    masks = [(token - lag * rows >= first).astype(F32) for lag in range(1, per + 1)]

    def gather(g, carry):
        for a in range(per):
            for lag in range(1, per + 1):
                keep = jnp.broadcast_to(masks[lag - 1][a:a + 1], (per_group, rows)).astype(BF16)
                xm[g, a * per_group:(a + 1) * per_group, (lag - 1) * rows:lag * rows] = (
                    xin[per + a - lag, part(g), :] * keep
                )
        return carry

    def begin(g, carry):
        far = jnp.dot(xm[g, :, 0:EARLY * rows], wfar[g, 0:EARLY * rows, :], preferred_element_type=F32) * reach
        near = w0[g]
        for a in range(per):
            own = jnp.dot(xin[per + a, part(g), :], near * diagmask[a], preferred_element_type=F32)
            here = slice(a * per_group, (a + 1) * per_group)
            acc[g, here] = far[here] + own
        return carry

    def finish(g, carry):
        far = jnp.dot(xm[g, :, EARLY * rows:], wfar[g, EARLY * rows:, :], preferred_element_type=F32)
        conv = far * reach + acc[g]
        sums = []
        for a in range(per):
            some = conv[a * per_group:(a + 1) * per_group] * qin[a, part(g), :].astype(F32)
            outbuf[a, part(g), :] = some.astype(BF16)
            sums.append(jnp.sum((some * some).reshape(per_group // 8, 8, rows), axis=0))
        return carry + jnp.stack(sums)

    for lag in range(EARLY + 1):
        if lag < planes:
            take(lag)
        lax.fori_loop(0, mine, partial(build, lag), 0, unroll=True)
    for copy in halo:
        pl.when(z > 0)(copy.wait_recv)
    lax.fori_loop(0, mine, gather, 0, unroll=True)
    lax.fori_loop(0, mine, begin, 0, unroll=True)
    for lag in range(EARLY + 1, per + 1):
        if lag < planes:
            take(lag)
        lax.fori_loop(0, mine, partial(build, lag), 0, unroll=True)
    for copy in asked:
        copy.wait_recv()
    power = lax.fori_loop(0, mine, finish, jnp.zeros((per, 8, rows), F32), unroll=True)

    pw[y] = jnp.sum(power, axis=1)
    shared = [
        send(pw.at[y], pw.at[y], p_s.at[d], p_r.at[d], (me, lax.rem(y + d, across))) for d in range(1, across)
    ]
    back = []
    for dx, dc, n in peers:
        to = place(dx, dc)
        back.append(send(outbuf.at[to], cin.at[j], o_s.at[n], o_r.at[n], in_plane(to)))
    cin[j] = outbuf[j]
    for copy in shared:
        copy.wait_recv()
    power = pw[0]
    for d in range(1, across):
        power = power + pw[d]
    for a in range(per):
        psend[a] = jnp.broadcast_to(power[a:a + 1], (8, rows))
    totals = []
    for dx, dc, n in peers:
        to = place(dx, dc)
        totals.append(send(psend.at[to, 0:1], precv.at[j, 0:1], t_s.at[n], t_r.at[n], in_plane(to)))
    precv[j] = psend[j]
    for copy, (dx, dc, n) in zip([None] + back, [(0, 0, 0)] + peers):
        if copy is not None:
            copy.wait_recv()
        origin = place(chips - dx, 2 - dc)
        cols = pl.ds(pl.multiple_of(origin * wide, wide), wide)
        gated[:, cols] = jnp.transpose(cin[origin].astype(F32))
    for copy in totals:
        copy.wait_recv()
    power = jnp.sum(precv[:, 0:1], axis=0)
    scale = lax.rsqrt(power / (width * across) + EPS)
    scale = jnp.transpose(jnp.broadcast_to(scale[0:1], (rows, rows)))
    loads[5].wait()
    for d in range(per):
        cols = slice(d * wide, (d + 1) * wide)
        weight = gain[cols].astype(F32).reshape(1, wide)
        out[:, cols] = (gated[:, cols] * scale * weight).astype(BF16)
    for copy in f1 + f2 + plane + asked + back + shared + totals:
        copy.wait_send()
    for copy in halo:
        pl.when(z < planes - 1)(copy.wait_send)


def shards(query, key_in, value, filt, gain, lengths):
    rows, width = query.shape
    taps, groups = filt.shape
    per = LONGEST // rows
    planes, across = lax.axis_size("ctx") // per, lax.axis_size("grp")
    mine, wide = groups // per, width // per
    sizes = (per, planes, across, rows, width, taps, lengths.shape[0])
    vmem, dma = pltpu.VMEM, pltpu.SemaphoreType.DMA
    return pl.pallas_call(
        partial(kernel, sizes),
        out_shape=jax.ShapeDtypeStruct((rows, width), BF16),
        in_specs=[pl.BlockSpec(memory_space=pltpu.HBM)] * 6,
        out_specs=pl.BlockSpec(memory_space=vmem),
        scratch_shapes=[
            pltpu.SMEM(lengths.shape, jnp.int32),
            vmem(filt.shape, BF16),
            vmem(gain.shape, BF16),
            vmem((rows, width), BF16),
            vmem((rows, width), BF16),
            vmem((rows, width), BF16),
            vmem((rows, rows), F32),
            vmem((per, mine, rows), F32),
            vmem((per, mine, rows), F32),
            vmem((planes, mine, rows), F32),
            vmem((mine, rows, rows), F32),
            vmem((per, wide, rows), BF16),
            vmem((2 * per, wide, rows), BF16),
            vmem((per, wide, rows), BF16),
            vmem((per, wide, rows), BF16),
            vmem((mine, per * rows, rows), BF16),
            vmem((mine, rows, rows), BF16),
            vmem((per, rows, rows), BF16),
            vmem((mine, per * (width // groups), per * rows), BF16),
            vmem((mine, per * (width // groups), rows), F32),
            vmem((per, wide, rows), BF16),
            vmem((per, wide, rows), BF16),
            vmem((rows, width), F32),
            vmem((across, per, rows), F32),
            vmem((per, 8, rows), F32),
            vmem((per, 8, rows), F32),
            dma((6,)),
            dma((per,)), dma((per,)),
            dma((planes,)), dma((planes,)),
            dma((per,)), dma((per,)),
            dma((per,)), dma((per,)),
            dma((per,)), dma((per,)),
            dma((per,)), dma((per,)),
            dma((across,)), dma((across,)),
            dma((per,)), dma((per,)),
            pltpu.SemaphoreType.REGULAR((planes,)),
        ],
        compiler_params=pltpu.CompilerParams(
            collective_id=0, has_side_effects=True, vmem_limit_bytes=50000 * 1024
        ),
    )(*(pltpu.with_memory_space_constraint(x, pltpu.HBM) for x in (lengths, filt, gain, query, key_in, value)))


def solution(mesh):
    placed = (P("ctx", "grp"), P("ctx", "grp"), P("ctx", "grp"), P("ctx", "grp"), P("grp"), P())
    return jax.shard_map(
        shards, mesh=mesh, in_specs=placed, out_specs=P("ctx", "grp"), check_vma=False
    )
```

```python
from functools import partial

import jax
import jax.numpy as jnp
from jax import lax
from jax.experimental import pallas as pl
from jax.experimental.pallas import tpu as pltpu
from jax.sharding import PartitionSpec as P

LONGEST = 1024
EARLY = 3
EPS = 1e-05
MESH = pl.DeviceIdType.MESH
BF16, F32 = jnp.bfloat16, jnp.float32


def kernel(
    sizes, lengths_hbm, filt_hbm, gain_hbm, query, key_in, value, out,
    lengths, filt, gain, q_buf, k_buf, v_buf, fpad, fsend, frecv, ff, turned, xsend, xin, qsend, qin, wfar, w0, diagmask, xm,
    acc, outbuf, cin, gated, psend, precv, load_sem,
    f1_s, f1_r, f2_s, f2_r, x_s, x_r, q_s, q_r, h_s, h_r, o_s, o_r, p_s, p_r, hello,
):
    per, planes, across, rows, width, taps, docs = sizes
    groups = filt.shape[1]
    mine, per_group = groups // per, width // groups
    wide = width // per
    me, y = lax.axis_index("ctx"), lax.axis_index("grp")
    z, j = me // per, me % per
    chip, core = j // 2, j % 2
    chips = per // 2

    def place(dx, dc):
        return lax.rem(chip + dx, chips) * 2 + lax.rem(core + dc, 2)

    def in_plane(to):
        return (z * per + to, y)

    def in_column(d):
        return (lax.rem(z + d, planes) * per + j, y)

    order = list(dict.fromkeys([0] + [dx for pair in zip(range(1, chips), range(chips - 1, 0, -1)) for dx in pair]))
    peers = [(dx, dc, dx * 2 + dc) for dx in order for dc in (0, 1)][1:]

    loads = [
        pltpu.make_async_copy(src, dst, load_sem.at[i])
        for i, (src, dst) in enumerate((
            (filt_hbm, filt), (key_in, k_buf), (value, v_buf), (lengths_hbm, lengths), (query, q_buf), (gain_hbm, gain)
        ))
    ]
    for load in loads:
        load.start()

    barrier = pltpu.get_barrier_semaphore()

    def greet(device):
        pl.semaphore_signal(barrier, inc=1, device_id=device, device_id_type=MESH)

    for dx, dc, _ in peers:
        greet(in_plane(place(dx, dc)))
    for d in range(1, across):
        greet((me, lax.rem(y + d, across)))
    greet(in_column(planes - 1))
    for d in range(1, planes - 1):
        pl.when(z + d < planes)(partial(greet, in_column(d)))
    greeted = (per - 1) + (across - 1) + z + jnp.where(z < planes - 1, 1, 0)

    fpad[...] = jnp.zeros_like(fpad)
    loads[0].wait()
    fpad[pl.ds(pl.multiple_of(j * taps, taps), taps), 0:groups] = filt[...].astype(F32)
    by_group = jnp.transpose(fpad[...])
    for d in range(per):
        fsend[d] = by_group[d * mine:(d + 1) * mine]

    loads[1].wait()
    loads[2].wait()
    for b in range(per):
        cols = slice(b * wide, (b + 1) * wide)
        signal = k_buf[:, cols].astype(F32) * v_buf[:, cols].astype(F32)
        xsend[b] = jnp.transpose(signal).astype(BF16)

    pl.semaphore_wait(barrier, greeted)

    def copy_to(src, dst, send_sem, recv_sem, device):
        return pltpu.make_async_remote_copy(
            src_ref=src, dst_ref=dst, send_sem=send_sem, recv_sem=recv_sem, device_id=device, device_id_type=MESH
        )

    def send(*what):
        copy = copy_to(*what)
        copy.start()
        return copy

    for d in range(1, planes):
        @pl.when(z >= d)
        def _():
            pl.semaphore_signal(hello.at[d], inc=1, device_id=in_column(planes - d), device_id_type=MESH)

    f1, plane = [], []
    for dx, dc, n in peers:
        to = place(dx, dc)
        f1.append(send(fsend.at[to], frecv.at[j], f1_s.at[n], f1_r.at[n], in_plane(to)))
    for dx, dc, n in peers:
        to = place(dx, dc)
        plane.append(send(xsend.at[to], xin.at[per + j], x_s.at[n], x_r.at[n], in_plane(to)))
    halo = [copy_to(xsend.at[j], xin.at[j], h_s.at[0], h_r.at[0], in_column(1))]
    for dx, dc, n in peers:
        origin = place(chips - dx, 2 - dc)
        halo.append(copy_to(xin.at[per + origin], xin.at[origin], h_s.at[n], h_r.at[n], in_column(1)))
    pl.when(z < planes - 1)(halo[0].start)
    xin[per + j] = xsend[j]
    frecv[j] = fsend[j]

    @pl.when(z == 0)
    def _():
        xin[0:per] = jnp.zeros((per, wide, rows), BF16)

    loads[3].wait()
    base = z * (per * rows)
    block = lax.broadcasted_iota(jnp.int32, (per, rows), 0)
    lane = lax.broadcasted_iota(jnp.int32, (per, rows), 1)
    ahead = base + block * rows
    token = ahead + lane
    end, start, first = jnp.int32(0), jnp.zeros_like(token), jnp.zeros_like(token)
    for m in range(docs):
        end = end + lengths[m]
        start = jnp.where(end <= token, end, start)
        first = jnp.where(end <= ahead, end, first)

    for copy in f1:
        copy.wait_recv()
    taps_here = frecv[0]
    for d in range(1, per):
        taps_here = taps_here + frecv[d]
    ff[z] = taps_here
    f2 = [copy_to(ff.at[z], ff.at[z], f2_s.at[d], f2_r.at[d], in_column(d)) for d in range(1, planes)]
    for d in range(1, planes):
        pl.when(z + d >= planes)(f2[d - 1].start)

    for copy, following in zip(plane, halo[1:]):
        copy.wait_recv()
        pl.when(z < planes - 1)(following.start)

    loads[4].wait()
    asked = []
    for b in range(per):
        cols = slice(b * wide, (b + 1) * wide)
        qsend[b] = jnp.transpose(q_buf[:, cols].astype(F32)).astype(BF16)
    for dx, dc, n in peers:
        to = place(dx, dc)
        asked.append(send(qsend.at[to], qin.at[j], q_s.at[n], q_r.at[n], in_plane(to)))
    qin[j] = qsend[j]

    reach = jnp.concatenate(
        [jnp.broadcast_to((start < ahead).astype(F32)[a:a + 1], (per_group, rows)) for a in range(per)], axis=0
    )
    source = lax.broadcasted_iota(jnp.int32, (rows, rows), 0)
    target = lax.broadcasted_iota(jnp.int32, (rows, rows), 1)
    causal = target >= source
    within = start - ahead
    for a in range(per):
        diagmask[a] = (source >= within[a:a + 1]).astype(F32).astype(BF16)

    for d in range(1, planes):
        @pl.when(z + d < planes)
        def _():
            pl.semaphore_wait(hello.at[d], 1)
            f2[d - 1].start()

    def take(other):
        @pl.when(z != other)
        def _():
            d = lax.rem(z - other + planes, planes)
            copy_to(ff.at[other], ff.at[other], f2_s.at[d], f2_r.at[d], in_column(d)).wait_recv()

    def build(lag, g, carry):
        if lag < planes:
            row = jnp.broadcast_to(ff[lag, pl.ds(g, 1), :], (rows, rows))
            now = pltpu.roll(row, 0, 1, stride=1, stride_axis=0)
        else:
            now = jnp.zeros((rows, rows), F32)
        if lag == 0:
            w0[g] = jnp.where(causal, now, 0.0).astype(BF16)
        else:
            wfar[g, (lag - 1) * rows:lag * rows, :] = jnp.where(causal, now, turned[g]).astype(BF16)
        turned[g] = now
        return carry

    def part(g):
        return pl.ds(pl.multiple_of(g * per_group, per_group), per_group)

    masks = [(token - lag * rows >= first).astype(F32) for lag in range(1, per + 1)]

    def gather(g, carry):
        for a in range(per):
            for lag in range(1, per + 1):
                keep = jnp.broadcast_to(masks[lag - 1][a:a + 1], (per_group, rows)).astype(BF16)
                xm[g, a * per_group:(a + 1) * per_group, (lag - 1) * rows:lag * rows] = (
                    xin[per + a - lag, part(g), :] * keep
                )
        return carry

    def begin(g, carry):
        far = jnp.dot(xm[g, :, 0:EARLY * rows], wfar[g, 0:EARLY * rows, :], preferred_element_type=F32) * reach
        near = w0[g]
        for a in range(per):
            own = jnp.dot(xin[per + a, part(g), :], near * diagmask[a], preferred_element_type=F32)
            here = slice(a * per_group, (a + 1) * per_group)
            acc[g, here] = far[here] + own
        return carry

    def finish(g, carry):
        far = jnp.dot(xm[g, :, EARLY * rows:], wfar[g, EARLY * rows:, :], preferred_element_type=F32)
        conv = far * reach + acc[g]
        sums = []
        for a in range(per):
            some = conv[a * per_group:(a + 1) * per_group] * qin[a, part(g), :].astype(F32)
            outbuf[a, part(g), :] = some.astype(BF16)
            sums.append(jnp.sum((some * some).reshape(per_group // 8, 8, rows), axis=0))
        return carry + jnp.stack(sums)

    for lag in range(EARLY + 1):
        if lag < planes:
            take(lag)
        lax.fori_loop(0, mine, partial(build, lag), 0, unroll=True)
    for copy in halo:
        pl.when(z > 0)(copy.wait_recv)
    lax.fori_loop(0, mine, gather, 0, unroll=True)
    lax.fori_loop(0, mine, begin, 0, unroll=True)
    for lag in range(EARLY + 1, per + 1):
        if lag < planes:
            take(lag)
        lax.fori_loop(0, mine, partial(build, lag), 0, unroll=True)
    for copy in asked:
        copy.wait_recv()
    power = lax.fori_loop(0, mine, finish, jnp.zeros((per, 8, rows), F32), unroll=True)

    power = jnp.sum(power, axis=1)
    for a in range(per):
        psend[a] = jnp.broadcast_to(power[a:a + 1], (8, rows))
    mark = y * per + j

    def tell(to, d):
        other = lax.rem(y + d, across)
        copy_to(psend.at[to, 0:1], precv.at[mark, 0:1], p_s.at[0], p_r.at[0], (z * per + to, other)).start()

    for d in sorted(range(across), key=lambda d: -min(d, across - d)):
        for dx, dc, n in [(0, 0, 0)] * (d > 0) + peers:
            tell(place(dx, dc), d)
    back = []
    for dx, dc, n in peers:
        to = place(dx, dc)
        back.append(send(outbuf.at[to], cin.at[j], o_s.at[n], o_r.at[n], in_plane(to)))
    cin[j] = outbuf[j]
    precv[mark] = psend[j]
    for copy, (dx, dc, n) in zip([None] + back, [(0, 0, 0)] + peers):
        if copy is not None:
            copy.wait_recv()
        origin = place(chips - dx, 2 - dc)
        cols = pl.ds(pl.multiple_of(origin * wide, wide), wide)
        gated[:, cols] = jnp.transpose(cin[origin].astype(F32))
    rest = precv.at[0:across * per - 1, 0:1]
    told = copy_to(rest, rest, p_s.at[0], p_r.at[0], in_plane(place(0, 1)))
    told.wait_recv()
    power = jnp.sum(precv[...], axis=0)
    scale = lax.rsqrt(power / (width * across) + EPS)
    scale = jnp.transpose(jnp.broadcast_to(scale[0:1], (rows, rows)))
    loads[5].wait()
    for d in range(per):
        cols = slice(d * wide, (d + 1) * wide)
        weight = gain[cols].astype(F32).reshape(1, wide)
        out[:, cols] = (gated[:, cols] * scale * weight).astype(BF16)
    for copy in f1 + f2 + plane + asked + back:
        copy.wait_send()
    told.wait_send()
    for copy in halo:
        pl.when(z < planes - 1)(copy.wait_send)


def shards(query, key_in, value, filt, gain, lengths):
    rows, width = query.shape
    taps, groups = filt.shape
    per = LONGEST // rows
    planes, across = lax.axis_size("ctx") // per, lax.axis_size("grp")
    mine, wide = groups // per, width // per
    sizes = (per, planes, across, rows, width, taps, lengths.shape[0])
    vmem, dma = pltpu.VMEM, pltpu.SemaphoreType.DMA
    return pl.pallas_call(
        partial(kernel, sizes),
        out_shape=jax.ShapeDtypeStruct((rows, width), BF16),
        in_specs=[pl.BlockSpec(memory_space=pltpu.HBM)] * 6,
        out_specs=pl.BlockSpec(memory_space=vmem),
        scratch_shapes=[
            pltpu.SMEM(lengths.shape, jnp.int32),
            vmem(filt.shape, BF16),
            vmem(gain.shape, BF16),
            vmem((rows, width), BF16),
            vmem((rows, width), BF16),
            vmem((rows, width), BF16),
            vmem((rows, rows), F32),
            vmem((per, mine, rows), F32),
            vmem((per, mine, rows), F32),
            vmem((planes, mine, rows), F32),
            vmem((mine, rows, rows), F32),
            vmem((per, wide, rows), BF16),
            vmem((2 * per, wide, rows), BF16),
            vmem((per, wide, rows), BF16),
            vmem((per, wide, rows), BF16),
            vmem((mine, per * rows, rows), BF16),
            vmem((mine, rows, rows), BF16),
            vmem((per, rows, rows), BF16),
            vmem((mine, per * (width // groups), per * rows), BF16),
            vmem((mine, per * (width // groups), rows), F32),
            vmem((per, wide, rows), BF16),
            vmem((per, wide, rows), BF16),
            vmem((rows, width), F32),
            vmem((per, 8, rows), F32),
            vmem((across * per, 8, rows), F32),
            dma((6,)),
            dma((per,)), dma((per,)),
            dma((planes,)), dma((planes,)),
            dma((per,)), dma((per,)),
            dma((per,)), dma((per,)),
            dma((per,)), dma((per,)),
            dma((per,)), dma((per,)),
            dma((1,)), dma((1,)),
            pltpu.SemaphoreType.REGULAR((planes,)),
        ],
        compiler_params=pltpu.CompilerParams(
            collective_id=0, has_side_effects=True, vmem_limit_bytes=50000 * 1024
        ),
    )(*(pltpu.with_memory_space_constraint(x, pltpu.HBM) for x in (lengths, filt, gain, query, key_in, value)))


def solution(mesh):
    placed = (P("ctx", "grp"), P("ctx", "grp"), P("ctx", "grp"), P("ctx", "grp"), P("grp"), P())
    return jax.shard_map(
        shards, mesh=mesh, in_specs=placed, out_specs=P("ctx", "grp"), check_vma=False
    )
```

```python
from functools import partial

import jax
import jax.numpy as jnp
from jax import lax
from jax.experimental import pallas as pl
from jax.experimental.pallas import tpu as pltpu
from jax.sharding import PartitionSpec as P

LONGEST = 1024
EARLY = 3
EPS = 1e-05
MESH = pl.DeviceIdType.MESH
BF16, F32 = jnp.bfloat16, jnp.float32


def kernel(
    sizes, lengths_hbm, filt_hbm, gain_hbm, query, key_in, value, out,
    lengths, filt, gain, q_buf, k_buf, v_buf, fpad, fsend, frecv, fnext, ff, fl, turned, xsend, xin, qsend, qin, wfar, w0, diagmask, xm,
    acc, outbuf, cin, gated, psend, precv, load_sem,
    s_s, s_r, f1_s, f1_r, f2_s, f2_r, x_s, x_r, q_s, q_r, h_s, h_r, o_s, o_r, p_s, p_r, hello,
):
    per, planes, across, rows, width, taps, docs = sizes
    groups = filt.shape[1]
    mine, per_group = groups // per, width // groups
    wide = width // per
    me, y = lax.axis_index("ctx"), lax.axis_index("grp")
    z, j = me // per, me % per
    chip, core = j // 2, j % 2
    chips = per // 2

    def place(dx, dc):
        return lax.rem(chip + dx, chips) * 2 + lax.rem(core + dc, 2)

    def in_plane(to):
        return (z * per + to, y)

    def in_column(d):
        return (lax.rem(z + d, planes) * per + j, y)

    order = list(dict.fromkeys([0] + [dx for pair in zip(range(1, chips), range(chips - 1, 0, -1)) for dx in pair]))
    peers = [(dx, dc, dx * 2 + dc) for dx in order for dc in (0, 1)][1:]

    loads = [
        pltpu.make_async_copy(src, dst, load_sem.at[i])
        for i, (src, dst) in enumerate((
            (filt_hbm, filt), (key_in, k_buf), (value, v_buf), (lengths_hbm, lengths), (query, q_buf), (gain_hbm, gain)
        ))
    ]
    for load in loads:
        load.start()

    barrier = pltpu.get_barrier_semaphore()

    def greet(device):
        pl.semaphore_signal(barrier, inc=1, device_id=device, device_id_type=MESH)

    for dx, dc, _ in peers:
        greet(in_plane(place(dx, dc)))
    for d in range(1, across):
        greet((me, lax.rem(y + d, across)))
    greet(in_column(planes - 1))
    for d in range(1, planes - 1):
        pl.when(z + d < planes)(partial(greet, in_column(d)))
    soon, late = 1, 1

    @pl.when(z < soon)
    def _():
        for other in range(late, planes):
            for dx, dc, _ in peers:
                greet((other * per + place(dx, dc), y))

    greeted = (per - 1) + (across - 1) + z + jnp.where(z < planes - 1, 1, 0) + jnp.where(z >= late, soon * (per - 1), 0)

    fpad[...] = jnp.zeros_like(fpad)
    loads[0].wait()
    fpad[0:taps, 0:groups] = filt[...].astype(F32)
    by_group = jnp.transpose(fpad[...])
    for d in range(per):
        spread = pltpu.roll(by_group[d * mine:(d + 1) * mine], 0, 1, stride=taps, stride_axis=0)
        fsend[d] = jnp.broadcast_to(jnp.sum(spread, axis=0, keepdims=True), (mine, rows))

    loads[1].wait()
    loads[2].wait()
    for b in range(per):
        cols = slice(b * wide, (b + 1) * wide)
        signal = k_buf[:, cols].astype(F32) * v_buf[:, cols].astype(F32)
        xsend[b] = jnp.transpose(signal).astype(BF16)

    pl.semaphore_wait(barrier, greeted)

    def copy_to(src, dst, send_sem, recv_sem, device):
        return pltpu.make_async_remote_copy(
            src_ref=src, dst_ref=dst, send_sem=send_sem, recv_sem=recv_sem, device_id=device, device_id_type=MESH
        )

    def send(*what):
        copy = copy_to(*what)
        copy.start()
        return copy

    for d in range(1, planes):
        @pl.when(z >= d)
        def _():
            pl.semaphore_signal(hello.at[d], inc=1, device_id=in_column(planes - d), device_id_type=MESH)

    f1, plane = [], []
    for dx, dc, n in peers:
        to = place(dx, dc)
        f1.append(send(fsend.at[to, 0:1], frecv.at[j, 0:1], f1_s.at[n], f1_r.at[n], in_plane(to)))

    def straight(other, to):
        return copy_to(fsend.at[to, 0:1], fnext.at[z, j, 0:1], s_s.at[other], s_r.at[z], (other * per + to, y))

    @pl.when(z >= late)
    def _():
        for other in range(soon):
            for to in range(per):
                straight(other, to).start()

    for dx, dc, n in peers:
        to = place(dx, dc)
        plane.append(send(xsend.at[to], xin.at[per + j], x_s.at[n], x_r.at[n], in_plane(to)))
    halo = [copy_to(xsend.at[j], xin.at[j], h_s.at[0], h_r.at[0], in_column(1))]
    for dx, dc, n in peers:
        origin = place(chips - dx, 2 - dc)
        halo.append(copy_to(xin.at[per + origin], xin.at[origin], h_s.at[n], h_r.at[n], in_column(1)))
    pl.when(z < planes - 1)(halo[0].start)
    xin[per + j] = xsend[j]
    frecv[j] = fsend[j]

    @pl.when(z == 0)
    def _():
        xin[0:per] = jnp.zeros((per, wide, rows), BF16)

    loads[3].wait()
    base = z * (per * rows)
    block = lax.broadcasted_iota(jnp.int32, (per, rows), 0)
    lane = lax.broadcasted_iota(jnp.int32, (per, rows), 1)
    ahead = base + block * rows
    token = ahead + lane
    end, start, first = jnp.int32(0), jnp.zeros_like(token), jnp.zeros_like(token)
    for m in range(docs):
        end = end + lengths[m]
        start = jnp.where(end <= token, end, start)
        first = jnp.where(end <= ahead, end, first)

    for copy in f1:
        copy.wait_recv()
    ff[z] = frecv[:, 0, :]
    f2 = [copy_to(ff.at[z], ff.at[z], f2_s.at[d], f2_r.at[d], in_column(d)) for d in range(1, planes)]
    for d in range(1, planes):
        lower = z + d - planes
        pl.when((lower >= soon) | ((lower >= 0) & (z < late)))(f2[d - 1].start)

    for copy, following in zip(plane, halo[1:]):
        copy.wait_recv()
        pl.when(z < planes - 1)(following.start)

    loads[4].wait()
    asked = []
    for b in range(per):
        cols = slice(b * wide, (b + 1) * wide)
        qsend[b] = jnp.transpose(q_buf[:, cols].astype(F32)).astype(BF16)
    for dx, dc, n in peers:
        to = place(dx, dc)
        asked.append(send(qsend.at[to], qin.at[j], q_s.at[n], q_r.at[n], in_plane(to)))
    qin[j] = qsend[j]

    reach = jnp.concatenate(
        [jnp.broadcast_to((start < ahead).astype(F32)[a:a + 1], (per_group, rows)) for a in range(per)], axis=0
    )
    source = lax.broadcasted_iota(jnp.int32, (rows, rows), 0)
    target = lax.broadcasted_iota(jnp.int32, (rows, rows), 1)
    causal = target >= source
    within = start - ahead
    for a in range(per):
        diagmask[a] = (source >= within[a:a + 1]).astype(F32).astype(BF16)

    for d in range(1, planes):
        @pl.when(z + d < planes)
        def _():
            pl.semaphore_wait(hello.at[d], 1)
            f2[d - 1].start()

    place_of = lax.broadcasted_iota(jnp.int32, (per, rows), 1) // taps
    own_place = place_of == lax.broadcasted_iota(jnp.int32, (per, rows), 0)

    def unpack(packed):
        some = []
        spread = pltpu.roll(packed, 0, 1, stride=taps, stride_axis=0)
        for g in range(mine):
            moved = pltpu.roll(spread, rows - g * taps, 1) if g else spread
            some.append(jnp.sum(jnp.where(own_place, moved, 0.0), axis=0, keepdims=True))
        return jnp.concatenate(some, axis=0)

    def take(other):
        def staged():
            d = lax.rem(z - other + planes, planes)
            copy_to(ff.at[other], ff.at[other], f2_s.at[d], f2_r.at[d], in_column(d)).wait_recv()
            fl[other] = unpack(ff[other])

        def direct():
            some = fnext.at[other, :, 0:1]
            copy_to(some, some, s_s.at[0], s_r.at[other], in_column(1)).wait_recv()
            fl[other] = unpack(fnext[other, :, 0, :])

        @pl.when(z == other)
        def _():
            fl[other] = unpack(ff[other])

        if other >= late:
            pl.when(z < soon)(direct)
            pl.when((z >= soon) & (z != other))(staged)
        else:
            pl.when(z != other)(staged)

    def build(lag, g, carry):
        if lag < planes:
            row = jnp.broadcast_to(fl[lag, pl.ds(g, 1), :], (rows, rows))
            now = pltpu.roll(row, 0, 1, stride=1, stride_axis=0)
        else:
            now = jnp.zeros((rows, rows), F32)
        if lag == 0:
            w0[g] = jnp.where(causal, now, 0.0).astype(BF16)
        else:
            wfar[g, (lag - 1) * rows:lag * rows, :] = jnp.where(causal, now, turned[g]).astype(BF16)
        turned[g] = now
        return carry

    def part(g):
        return pl.ds(pl.multiple_of(g * per_group, per_group), per_group)

    masks = [(token - lag * rows >= first).astype(F32) for lag in range(1, per + 1)]

    def gather(g, carry):
        for a in range(per):
            for lag in range(1, per + 1):
                keep = jnp.broadcast_to(masks[lag - 1][a:a + 1], (per_group, rows)).astype(BF16)
                xm[g, a * per_group:(a + 1) * per_group, (lag - 1) * rows:lag * rows] = (
                    xin[per + a - lag, part(g), :] * keep
                )
        return carry

    def begin(g, carry):
        far = jnp.dot(xm[g, :, 0:EARLY * rows], wfar[g, 0:EARLY * rows, :], preferred_element_type=F32) * reach
        near = w0[g]
        for a in range(per):
            own = jnp.dot(xin[per + a, part(g), :], near * diagmask[a], preferred_element_type=F32)
            here = slice(a * per_group, (a + 1) * per_group)
            acc[g, here] = far[here] + own
        return carry

    def finish(g, carry):
        far = jnp.dot(xm[g, :, EARLY * rows:], wfar[g, EARLY * rows:, :], preferred_element_type=F32)
        conv = far * reach + acc[g]
        sums = []
        for a in range(per):
            some = conv[a * per_group:(a + 1) * per_group] * qin[a, part(g), :].astype(F32)
            outbuf[a, part(g), :] = some.astype(BF16)
            sums.append(jnp.sum((some * some).reshape(per_group // 8, 8, rows), axis=0))
        return carry + jnp.stack(sums)

    for lag in range(EARLY + 1):
        if lag < planes:
            take(lag)
        lax.fori_loop(0, mine, partial(build, lag), 0, unroll=True)
    for copy in halo:
        pl.when(z > 0)(copy.wait_recv)
    lax.fori_loop(0, mine, gather, 0, unroll=True)
    lax.fori_loop(0, mine, begin, 0, unroll=True)
    for lag in range(EARLY + 1, per + 1):
        if lag < planes:
            take(lag)
        lax.fori_loop(0, mine, partial(build, lag), 0, unroll=True)
    for copy in asked:
        copy.wait_recv()
    power = lax.fori_loop(0, mine, finish, jnp.zeros((per, 8, rows), F32), unroll=True)

    power = jnp.sum(power, axis=1)
    for a in range(per):
        psend[a] = jnp.broadcast_to(power[a:a + 1], (8, rows))
    mark = y * per + j

    def tell(to, d):
        other = lax.rem(y + d, across)
        copy_to(psend.at[to, 0:1], precv.at[mark, 0:1], p_s.at[0], p_r.at[0], (z * per + to, other)).start()

    for d in sorted(range(across), key=lambda d: -min(d, across - d)):
        for dx, dc, n in [(0, 0, 0)] * (d > 0) + peers:
            tell(place(dx, dc), d)
    back = []
    for dx, dc, n in peers:
        to = place(dx, dc)
        back.append(send(outbuf.at[to], cin.at[j], o_s.at[n], o_r.at[n], in_plane(to)))
    cin[j] = outbuf[j]
    precv[mark] = psend[j]
    for copy, (dx, dc, n) in zip([None] + back, [(0, 0, 0)] + peers):
        if copy is not None:
            copy.wait_recv()
        origin = place(chips - dx, 2 - dc)
        cols = pl.ds(pl.multiple_of(origin * wide, wide), wide)
        gated[:, cols] = jnp.transpose(cin[origin].astype(F32))
    rest = precv.at[0:across * per - 1, 0:1]
    told = copy_to(rest, rest, p_s.at[0], p_r.at[0], in_plane(place(0, 1)))
    told.wait_recv()
    power = jnp.sum(precv[...], axis=0)
    scale = lax.rsqrt(power / (width * across) + EPS)
    scale = jnp.transpose(jnp.broadcast_to(scale[0:1], (rows, rows)))
    loads[5].wait()
    for d in range(per):
        cols = slice(d * wide, (d + 1) * wide)
        weight = gain[cols].astype(F32).reshape(1, wide)
        out[:, cols] = (gated[:, cols] * scale * weight).astype(BF16)
    for d in range(1, planes):
        lower = z + d - planes
        pl.when((lower < 0) | (lower >= soon) | (z < late))(f2[d - 1].wait_send)

    @pl.when(z >= late)
    def _():
        for other in range(soon):
            some = fsend.at[:, 0:1]
            copy_to(some, some, s_s.at[other], s_r.at[0], in_column(1)).wait_send()

    for copy in f1 + plane + asked + back:
        copy.wait_send()
    told.wait_send()
    for copy in halo:
        pl.when(z < planes - 1)(copy.wait_send)


def shards(query, key_in, value, filt, gain, lengths):
    rows, width = query.shape
    taps, groups = filt.shape
    per = LONGEST // rows
    planes, across = lax.axis_size("ctx") // per, lax.axis_size("grp")
    mine, wide = groups // per, width // per
    sizes = (per, planes, across, rows, width, taps, lengths.shape[0])
    vmem, dma = pltpu.VMEM, pltpu.SemaphoreType.DMA
    return pl.pallas_call(
        partial(kernel, sizes),
        out_shape=jax.ShapeDtypeStruct((rows, width), BF16),
        in_specs=[pl.BlockSpec(memory_space=pltpu.HBM)] * 6,
        out_specs=pl.BlockSpec(memory_space=vmem),
        scratch_shapes=[
            pltpu.SMEM(lengths.shape, jnp.int32),
            vmem(filt.shape, BF16),
            vmem(gain.shape, BF16),
            vmem((rows, width), BF16),
            vmem((rows, width), BF16),
            vmem((rows, width), BF16),
            vmem((rows, rows), F32),
            vmem((per, mine, rows), F32),
            vmem((per, mine, rows), F32),
            vmem((planes, per, mine, rows), F32),
            vmem((planes, mine, rows), F32),
            vmem((planes, mine, rows), F32),
            vmem((mine, rows, rows), F32),
            vmem((per, wide, rows), BF16),
            vmem((2 * per, wide, rows), BF16),
            vmem((per, wide, rows), BF16),
            vmem((per, wide, rows), BF16),
            vmem((mine, per * rows, rows), BF16),
            vmem((mine, rows, rows), BF16),
            vmem((per, rows, rows), BF16),
            vmem((mine, per * (width // groups), per * rows), BF16),
            vmem((mine, per * (width // groups), rows), F32),
            vmem((per, wide, rows), BF16),
            vmem((per, wide, rows), BF16),
            vmem((rows, width), F32),
            vmem((per, 8, rows), F32),
            vmem((across * per, 8, rows), F32),
            dma((6,)),
            dma((planes,)), dma((planes,)),
            dma((per,)), dma((per,)),
            dma((planes,)), dma((planes,)),
            dma((per,)), dma((per,)),
            dma((per,)), dma((per,)),
            dma((per,)), dma((per,)),
            dma((per,)), dma((per,)),
            dma((1,)), dma((1,)),
            pltpu.SemaphoreType.REGULAR((planes,)),
        ],
        compiler_params=pltpu.CompilerParams(
            collective_id=0, has_side_effects=True, vmem_limit_bytes=50000 * 1024
        ),
    )(*(pltpu.with_memory_space_constraint(x, pltpu.HBM) for x in (lengths, filt, gain, query, key_in, value)))


def solution(mesh):
    placed = (P("ctx", "grp"), P("ctx", "grp"), P("ctx", "grp"), P("ctx", "grp"), P("grp"), P())
    return jax.shard_map(
        shards, mesh=mesh, in_specs=placed, out_specs=P("ctx", "grp"), check_vma=False
    )
```
